256 devices in a mesh: cells: 16 (over z_hi, x, core), modes: 16 (over y, z_lo).
Axes of the slice: x: 4, y: 4, z: 8 (z_hi: 2, z_lo: 4; z = z_hi * 4 + z_lo), core: 2. Of those that a mesh axis runs over, the one named last changes fastest.
Arguments:
- hermite_coefficient_array: float32 [32, 64, 32, 2048], P('cells', None, None, 'modes'), may hold values from -6 to 6
- encounter_kernel_array: bfloat16 [14400, 120], replicated, may hold values from -0.046875 to 0.046875
- obstacle_indicator: int32 [32, 64, 32], P('cells'), may hold values 0 or 1
Outputs:
- moments_next: float32 [32, 64, 32, 2048], P('cells', None, None, 'modes')
The draws below stay inside these ranges and needn't reach their ends.
All inputs are finite; a program needn't handle non-finite values. No bound on the sum of `obstacle_indicator` on one device may be relied on, other than what follows from the above.
Results may differ from the reference program's by a relative error of at most 0.0003.
Values sent between devices are 32-bit elements; how exact they have to be, the bound alone decides.
No kernel may reach another device: no remote copies, remote signals or barrier semaphores. Data moves between devices by JAX's collectives and lax.ppermute only.
A program may use at most 64 MiB of HBM per device.

```python
import math
import jax
import jax.numpy as jnp
from jax import lax

NY = 64
NZ = 32
MA = 16
MB = 16
MC = 8
LDEG = 7
BASIS_SIZE = 120
MODES = 2048
NX = 32


def plant(array, own_key, smallest, largest):
    extent = array.shape
    index_at = [jax.random.randint(jax.random.fold_in(own_key, axis), (), 0, extent[axis]) for axis in range(len(extent))]
    array = array.at[tuple(index_at)].set(smallest)
    longest = extent.index(max(extent))
    index_at[longest] = (index_at[longest] + 1) % extent[longest]
    return array.at[tuple(index_at)].set(largest)


def block_levels(own_key, dims, shards, least, high):
    level, own = 1.0, jax.random.fold_in(own_key, 6)
    for position, parts in shards:
        heights = jnp.exp(jax.random.uniform(jax.random.fold_in(own, position), (parts,), jnp.float32, least / len(shards), high / len(shards)))
        level = level * jnp.repeat(heights, dims[position] // parts).reshape([-1 if axis == position else 1 for axis in range(len(dims))])
    return level


def normal_values(key, shape, deviation, limit, shards=(), held_as=jnp.bfloat16):
    entries = deviation * jax.random.normal(key, shape, jnp.float32)
    if shards:
        entries = entries * block_levels(key, shape, shards, -0.22, 0.18)
    return jnp.clip(entries, -limit, limit).astype(held_as)


def setup_inputs(seed: int = 0) -> dict:
    key_list = jax.random.split(jax.random.key(seed), 4)
    return {
        "hermite_coefficient_array": normal_values(key_list[0], (NX, NY, NZ, MODES), 1.0, 6.0, ((0, 16), (3, 16)), jnp.float32),
        "encounter_kernel_array": normal_values(key_list[1], (BASIS_SIZE * BASIS_SIZE, BASIS_SIZE), (BASIS_SIZE * BASIS_SIZE) ** -0.5, 0.046875),
        "obstacle_indicator": plant((jax.random.randint(key_list[2], (NX, NY, NZ), 0, 8) < 1).astype(jnp.int32), jax.random.fold_in(key_list[2], 1), 0, 1),
    }


CFL = 0.04
DTC = 0.2

def ladder_ref(field, axis):
    count = field.shape[axis]
    pad_spec = [(0, 0)] * field.ndim
    pad_spec[axis] = (1, 1)
    padded = jnp.pad(field, pad_spec)
    lower_part = lax.slice_in_dim(padded, 0, count, axis=axis)
    upper_part = lax.slice_in_dim(padded, 2, count + 2, axis=axis)
    shape_list = [1] * field.ndim
    shape_list[axis] = count
    level = jnp.arange(count, dtype=jnp.float32).reshape(shape_list)
    return jnp.sqrt(level) * lower_part + jnp.sqrt(level + 1.0) * upper_part

def transport(grid, obstacle_indicator):
    speed_x = 2.0 * math.sqrt(MA)
    speed_y = 2.0 * math.sqrt(MB)
    speed_z = 2.0 * math.sqrt(MC)

    def plane(plane_index):
        center = lax.dynamic_index_in_dim(grid, plane_index, 0, keepdims=False)
        behind = lax.dynamic_index_in_dim(grid, jnp.mod(plane_index - 1, NX), 0, keepdims=False)
        beyond = lax.dynamic_index_in_dim(grid, jnp.mod(plane_index + 1, NX), 0, keepdims=False)
        solid = lax.dynamic_index_in_dim(obstacle_indicator, plane_index, 0, keepdims=False)
        first_axis_gradient = beyond - behind
        lap_x = beyond - 2.0 * center + behind
        next_y = jnp.roll(center, -1, 0)
        prev_y = jnp.roll(center, 1, 0)
        next_z = jnp.roll(center, -1, 1)
        prev_z = jnp.roll(center, 1, 1)
        diff_y = next_y - prev_y
        lap_y = next_y - 2.0 * center + prev_y
        diff_z = next_z - prev_z
        lap_z = next_z - 2.0 * center + prev_z
        shaped = (NY, NZ, MA, MB, MC)
        flux = ladder_ref(first_axis_gradient.reshape(shaped), 2) + ladder_ref(diff_y.reshape(shaped), 3) + ladder_ref(diff_z.reshape(shaped), 4)
        flux = flux.reshape(NY, NZ, MODES)
        update = center + CFL * (-0.5 * flux + 0.5 * (speed_x * lap_x + speed_y * lap_y + speed_z * lap_z))
        return jnp.where(solid[..., None] != 0, center, update)
    return lax.map(plane, jnp.arange(NX, dtype=jnp.int32))

def reference(hermite_coefficient_array, encounter_kernel_array, obstacle_indicator):
    grid = hermite_coefficient_array
    for repeat in range(2):
        grid = transport(grid, obstacle_indicator)
    rows = grid.reshape(NX * NY * NZ, MODES)
    mode_index = jnp.arange(MODES, dtype=jnp.int32)
    degree = mode_index // (MB * MC) + mode_index // MC % MB + mode_index % MC
    low_index = jnp.nonzero(degree <= LDEG, size=BASIS_SIZE)[0].astype(jnp.int32)
    low = rows[:, low_index]

    def collide(block_rows):
        quadratic_factors = (block_rows[:, :, None] * block_rows[:, None, :]).reshape(block_rows.shape[0], BASIS_SIZE * BASIS_SIZE).astype(jnp.bfloat16)
        return jnp.dot(quadratic_factors, encounter_kernel_array, preferred_element_type=jnp.float32)
    scattered_state = lax.map(collide, low.reshape(-1, 512, BASIS_SIZE)).reshape(-1, BASIS_SIZE)
    rows = rows.at[:, low_index].add(DTC * scattered_state)
    return rows.reshape(NX, NY, NZ, MODES)
```

```python
import functools
import math

import jax
import jax.numpy as jnp
import numpy as np
from jax import lax
from jax.experimental import pallas as pl
from jax.experimental.pallas import tpu as pltpu
from jax.sharding import Mesh, PartitionSpec as P

MA = 16
MB = 16
MC = 8
LDEG = 7
BASIS_SIZE = 120
LANES = MB * MC
LOW_A = LDEG + 1
PAD = 128
CFL = 0.04
DTC = 0.2
HALF = 0.5 * CFL
CX = HALF * 2.0 * math.sqrt(MA)
CY = HALF * 2.0 * math.sqrt(MB)
CZ = HALF * 2.0 * math.sqrt(MC)
CENTER = 2.0 * (CX + CY + CZ)
ROWS = 8
COLS = 8
GROUP = 8

AXES = ("half", "column", "core", "row", "run")
SIZES = (2, 4, 2, 4, 4)


def pairs(move):
    out = []
    for source in np.ndindex(*SIZES):
        target = move(*source)
        out.append((int(np.ravel_multi_index(source, SIZES)), int(np.ravel_multi_index(target, SIZES))))
    return out


def along_x(by):
    def move(half, column, core, row, run):
        place = (column * 2 + core + by) % 8
        return (half, place // 2, place % 2, row, run)

    return pairs(move)


def along_y(by):
    def move(half, column, core, row, run):
        place = (half * 4 + run + by) % 8
        return (place // 4, column, core, row, place % 4)

    return pairs(move)


def along_z(by):
    return pairs(lambda half, column, core, row, run: (half, column, core, (row + by) % 4, run))


def other_half():
    return pairs(lambda half, column, core, row, run: (1 - half, column, core, row, run))


def send(value, route):
    return lax.ppermute(value, AXES, route)


def ladder_rows():
    lane = lax.broadcasted_iota(jnp.int32, (COLS, LANES), 1)
    b = lane // MC
    c = lane % MC
    b_low = HALF * jnp.sqrt(b.astype(jnp.float32))
    b_high = jnp.where(b < MB - 1, HALF * jnp.sqrt((b + 1).astype(jnp.float32)), 0.0)
    c_low = HALF * jnp.sqrt(c.astype(jnp.float32))
    c_high = jnp.where(c < MC - 1, HALF * jnp.sqrt((c + 1).astype(jnp.float32)), 0.0)
    return b_low, b_high, c_low, c_high


def advance(flags, first, second, x_back, x_next, y_back, y_next, z_back, z_next, open_cells, put):
    b_low, b_high, c_low, c_high = ladder_rows()
    depth = lax.broadcasted_iota(jnp.int32, (COLS, LANES), 0)
    at_start = depth == 0
    at_end = depth == COLS - 1

    def block(g, carry):
        g_back = jnp.where(flags[0] != 0, 1 - g, g)
        g_next = jnp.where(flags[1] != 0, 1 - g, g)
        for p in range(2):
            here = (first, second)[p]
            for y in range(ROWS):

                def sides(a):
                    if p == 0:
                        back = x_back[g_back, a, y]
                        ahead = second[g, a, y]
                    else:
                        back = first[g, a, y]
                        ahead = x_next[g_next, a, y]
                    return ahead - back, ahead + back

                is_open = open_cells[g, p, y]
                before = None
                now = sides(0)
                for a in range(MA):
                    after = sides(a + 1) if a + 1 < MA else None
                    f = here[g, a, y]
                    yb = here[g, a, y - 1] if y > 0 else y_back[g, a, p]
                    yn = here[g, a, y + 1] if y + 1 < ROWS else y_next[g, a, p]
                    zb = jnp.where(at_start, z_back[g, a, p, y : y + 1, :], pltpu.roll(f, 1, 0))
                    zn = jnp.where(at_end, z_next[g, a, p, y : y + 1, :], pltpu.roll(f, COLS - 1, 0))
                    dy = yn - yb
                    dz = zn - zb
                    change = CX * now[1] + CY * (yn + yb) + CZ * (zn + zb) - CENTER * f
                    if before is not None:
                        change = change - (HALF * math.sqrt(a)) * before
                    if after is not None:
                        change = change - (HALF * math.sqrt(a + 1)) * after[0]
                    change = change - b_low * pltpu.roll(dy, MC, 1)
                    change = change - b_high * pltpu.roll(dy, LANES - MC, 1)
                    change = change - c_low * pltpu.roll(dz, 1, 1)
                    change = change - c_high * pltpu.roll(dz, LANES - 1, 1)
                    put(g, a, p, y, f + is_open * change)
                    before = now[0]
                    now = after
        return carry

    lax.fori_loop(0, 2, block, 0)


def first_kernel(
    flags, first, second, x_back, x_next, y_back, y_next, z_back, z_next, open_cells,
    out_first, out_second, out_y0, out_y7, out_z0, out_z7,
):
    def put(g, a, p, y, value):
        (out_first, out_second)[p][g, a, y] = value
        if y == 0:
            out_y0[g, a, p] = value
        if y == ROWS - 1:
            out_y7[g, a, p] = value
        out_z0[g, a, p, y : y + 1, :] = value[0:1]
        out_z7[g, a, p, y : y + 1, :] = value[COLS - 1 : COLS]

    advance(flags, first, second, x_back, x_next, y_back, y_next, z_back, z_next, open_cells, put)


def three_parts(value):
    high = value.astype(jnp.bfloat16)
    rest = value - high.astype(jnp.float32)
    middle = rest.astype(jnp.bfloat16)
    low = (rest - middle.astype(jnp.float32)).astype(jnp.bfloat16)
    return high, middle, low


def second_kernel(
    flags, first, second, x_back, x_next, y_back, y_next, z_back, z_next, open_cells,
    selector, weights, out, low, factors,
):
    def put(g, a, p, y, value):
        out[g, a, p, y] = value

    advance(flags, first, second, x_back, x_next, y_back, y_next, z_back, z_next, open_cells, put)
    cells = 2 * 2 * ROWS * COLS

    def plane(a):
        parts = [out[g, a, p].reshape(ROWS * COLS, LANES) for g in range(2) for p in range(2)]
        return jnp.concatenate(parts, 0)

    picked = jnp.zeros((PAD, cells), jnp.float32)
    for a in range(LOW_A):
        for part in three_parts(plane(a)):
            picked = picked + lax.dot_general(
                selector[a], part, (((1,), (1,)), ((), ())), preferred_element_type=jnp.float32
            )
    low[...] = picked

    def collide(step, total):
        base = step * GROUP
        for i in range(GROUP):
            row = low[pl.ds(base + i, 1), :]
            factors[i * PAD : (i + 1) * PAD, :] = (low[...] * row).astype(jnp.bfloat16)
        columns = pl.ds(pl.multiple_of(base * PAD, GROUP * PAD), GROUP * PAD)
        return total + jnp.dot(weights[:, columns], factors[...], preferred_element_type=jnp.float32)

    rate = lax.fori_loop(0, BASIS_SIZE // GROUP, collide, jnp.zeros((PAD, cells), jnp.float32))
    rate_parts = three_parts(jnp.transpose(DTC * rate))
    for a in range(LOW_A):
        lifted = jnp.zeros((cells, LANES), jnp.float32)
        for part in rate_parts:
            lifted = lifted + jnp.dot(part, selector[a], preferred_element_type=jnp.float32)
        for g in range(2):
            for p in range(2):
                at = (g * 2 + p) * ROWS * COLS
                block = lifted[at : at + ROWS * COLS].reshape(ROWS, COLS, LANES)
                out[g, a, p] = out[g, a, p] + block


def low_selector():
    rank = 0
    table = np.zeros((LOW_A, PAD, LANES), np.float32)
    for a in range(MA):
        for b in range(MB):
            for c in range(MC):
                if a + b + c <= LDEG:
                    table[a, rank, b * MC + c] = 1.0
                    rank += 1
    return jnp.asarray(table, jnp.bfloat16)


VMEM = pl.BlockSpec(memory_space=pltpu.VMEM)
SMEM = pl.BlockSpec(memory_space=pltpu.SMEM)
PARAMS = pltpu.CompilerParams(vmem_limit_bytes=48 << 20)


def f32(*shape):
    return jax.ShapeDtypeStruct(shape, jnp.float32)


def halos(first, second, y0, y7, z0, z7):
    x_back = send(second, along_x(1))
    x_next = send(first, along_x(-1))
    y_back = send(y7, along_y(1))
    y_next = send(y0, along_y(-1))
    z_back = send(z7, along_z(1))
    z_next = send(z0, along_z(-1))
    return x_back, x_next, y_back, y_next, z_back, z_next


def body(field, kernel_table, obstacles):
    half = lax.axis_index("half")
    place = lax.axis_index("column") * 2 + lax.axis_index("core")
    flags = jnp.stack([place == 0, place == 7]).astype(jnp.int32)

    run = lax.axis_index("run")
    row = lax.axis_index("row")
    tiles = obstacles.reshape(2, 2, 4, ROWS, 4, COLS)
    tiles = lax.dynamic_index_in_dim(tiles, run, 2, keepdims=False)
    tiles = lax.dynamic_index_in_dim(tiles, row, 3, keepdims=False)
    gas = (tiles == 0).astype(jnp.float32)
    mine = lax.dynamic_index_in_dim(gas, half, 1, keepdims=False)
    for_other = lax.dynamic_index_in_dim(gas, 1 - half, 1, keepdims=False)
    theirs = send(for_other, other_half())
    both = jnp.where(half == 0, jnp.stack([mine, theirs]), jnp.stack([theirs, mine]))
    open_cells = jnp.broadcast_to(both[..., None], (2, 2, ROWS, COLS, LANES))

    blocks = field.reshape(2, 2, 4, ROWS, 4, COLS, LANES).transpose(1, 4, 2, 0, 3, 5, 6)
    blocks = blocks.reshape(32, 2, ROWS, COLS, LANES)
    state = lax.all_to_all(blocks, ("half", "row", "run"), 0, 0, tiled=True)
    state = state.reshape(2, MA, 2, ROWS, COLS, LANES)

    first = state[:, :, 0]
    second = state[:, :, 1]
    edges = (state[:, :, :, 0], state[:, :, :, ROWS - 1], state[..., 0, :], state[..., COLS - 1, :])
    around = halos(first, second, *edges)
    plane = f32(2, MA, ROWS, COLS, LANES)
    edge = f32(2, MA, 2, ROWS, LANES)
    first, second, *edges = pl.pallas_call(
        first_kernel,
        out_shape=(plane, plane, edge, edge, edge, edge),
        in_specs=[SMEM] + [VMEM] * 9,
        out_specs=(VMEM,) * 6,
        compiler_params=PARAMS,
    )(flags, first, second, *around, open_cells)

    around = halos(first, second, *edges)
    weights = kernel_table.reshape(BASIS_SIZE, BASIS_SIZE, BASIS_SIZE).transpose(2, 0, 1)
    weights = jnp.pad(weights, ((0, PAD - BASIS_SIZE), (0, 0), (0, PAD - BASIS_SIZE)))
    weights = weights.reshape(PAD, BASIS_SIZE * PAD)
    cells = 2 * 2 * ROWS * COLS
    state = pl.pallas_call(
        second_kernel,
        out_shape=f32(2, MA, 2, ROWS, COLS, LANES),
        in_specs=[SMEM] + [VMEM] * 11,
        out_specs=VMEM,
        scratch_shapes=[pltpu.VMEM((PAD, cells), jnp.float32), pltpu.VMEM((GROUP * PAD, cells), jnp.bfloat16)],
        compiler_params=PARAMS,
    )(flags, first, second, *around, open_cells, low_selector(), weights)

    back = lax.all_to_all(
        state.reshape(32, 2, ROWS, COLS, LANES), ("half", "row", "run"), 0, 0, tiled=True
    )
    back = back.reshape(2, 4, 4, 2, ROWS, COLS, LANES).transpose(3, 0, 2, 4, 1, 5, 6)
    return back.reshape(2, 64, 32, LANES)


def solution(mesh):
    named = Mesh(mesh.devices.reshape(SIZES), AXES)
    cells = ("half", "column", "core")
    modes = ("row", "run")
    placed = (P(cells, None, None, modes), P(), P(cells, None, None))
    return jax.shard_map(
        body, mesh=named, in_specs=placed, out_specs=P(cells, None, None, modes), check_vma=False
    )
```

```python
import functools
import math

import jax
import jax.numpy as jnp
import numpy as np
from jax import lax
from jax.experimental import pallas as pl
from jax.experimental.pallas import tpu as pltpu
from jax.sharding import Mesh, PartitionSpec as P

MA = 16
MB = 16
MC = 8
LDEG = 7
BASIS_SIZE = 120
LANES = MB * MC
LOW_A = LDEG + 1
PAD = 128
CFL = 0.04
DTC = 0.2
HALF = 0.5 * CFL
CX = HALF * 2.0 * math.sqrt(MA)
CY = HALF * 2.0 * math.sqrt(MB)
CZ = HALF * 2.0 * math.sqrt(MC)
CENTER = 2.0 * (CX + CY + CZ)
ROWS = 8
COLS = 8
GROUP = 16
BLOCKS = 32

AXES = ("half", "column", "core", "row", "run")
SIZES = (2, 4, 2, 4, 4)


def pairs(move):
    out = []
    for source in np.ndindex(*SIZES):
        target = move(*source)
        out.append((int(np.ravel_multi_index(source, SIZES)), int(np.ravel_multi_index(target, SIZES))))
    return out


def outer():
    def move(half, column, core, row, run):
        place = (column * 2 + core + (1 if core else -1)) % 8
        return (half, place // 2, place % 2, row, run)

    return pairs(move)


def inner():
    return pairs(lambda half, column, core, row, run: (half, column, 1 - core, row, run))


def along_y(by):
    def move(half, column, core, row, run):
        place = (half * 4 + run + by) % 8
        return (place // 4, column, core, row, place % 4)

    return pairs(move)


def along_z(by):
    return pairs(lambda half, column, core, row, run: (half, column, core, (row + by) % 4, run))


def other_half():
    return pairs(lambda half, column, core, row, run: (1 - half, column, core, row, run))


def send(value, route):
    return lax.ppermute(value, AXES, route)


def ladder_rows():
    lane = lax.broadcasted_iota(jnp.int32, (COLS, LANES), 1)
    b = lane // MC
    c = lane % MC
    b_low = HALF * jnp.sqrt(b.astype(jnp.float32))
    b_high = jnp.where(b < MB - 1, HALF * jnp.sqrt((b + 1).astype(jnp.float32)), 0.0)
    c_low = HALF * jnp.sqrt(c.astype(jnp.float32))
    c_high = jnp.where(c < MC - 1, HALF * jnp.sqrt((c + 1).astype(jnp.float32)), 0.0)
    return b_low, b_high, c_low, c_high


def advance(swap, steps, here, beside, beyond, y_back, y_next, z_back, z_next, open_cells, put):
    b_low, b_high, c_low, c_high = ladder_rows()
    depth = lax.broadcasted_iota(jnp.int32, (COLS, LANES), 0)
    at_start = depth == 0
    at_end = depth == COLS - 1

    def block(g, carry):
        far = g if swap is None else jnp.where(swap, 1 - g, g)
        for y in range(ROWS):

            def sides(a):
                near = beside[g, a, y]
                other = beyond[far, a, y]
                return near - other, near + other

            is_open = open_cells[g, y]
            before = None
            now = sides(0)
            for a in range(MA):
                after = sides(a + 1) if a + 1 < MA else None
                f = here[g, a, y]
                yb = here[g, a, y - 1] if y > 0 else y_back[g, a]
                yn = here[g, a, y + 1] if y + 1 < ROWS else y_next[g, a]
                zb = jnp.where(at_start, z_back[g, a, y : y + 1, :], pltpu.roll(f, 1, 0))
                zn = jnp.where(at_end, z_next[g, a, y : y + 1, :], pltpu.roll(f, COLS - 1, 0))
                dy = yn - yb
                dz = zn - zb
                change = CX * (now[1] + (yn + yb)) + CZ * (zn + zb) - CENTER * f
                if before is not None:
                    change = change - steps[a] * before
                if after is not None:
                    change = change - steps[a + 1] * after[0]
                change = change - b_low * pltpu.roll(dy, MC, 1)
                change = change - b_high * pltpu.roll(dy, LANES - MC, 1)
                change = change - c_low * pltpu.roll(dz, 1, 1)
                change = change - c_high * pltpu.roll(dz, LANES - 1, 1)
                put(g, a, y, f + is_open * change)
                before = now[0]
                now = after
        return carry

    lax.fori_loop(0, 2, block, 0)


def put_edges(g, a, y, value, out_y0, out_y7, out_z0, out_z7):
    if y == 0:
        out_y0[g, a] = value
    if y == ROWS - 1:
        out_y7[g, a] = value
    out_z0[g, a, y : y + 1, :] = value[0:1]
    out_z7[g, a, y : y + 1, :] = value[COLS - 1 : COLS]


def split_kernel(state, out_outer, out_inner, *edges):
    def block(index, carry):
        g = index // MA
        a = index % MA
        for which, out in enumerate((out_outer, out_inner)):
            for y in range(ROWS):
                value = state[g, a, which, y]
                out[g, a, y] = value
                put_edges(g, a, y, value, *[edge.at[which] for edge in edges])
        return carry

    lax.fori_loop(0, 2 * MA, block, 0)


def open_table(mine, theirs, table):
    half = lax.axis_index("half")
    cols = pl.ds(pl.multiple_of(lax.axis_index("row") * COLS, COLS), COLS)
    first_row = (half * 4 + lax.axis_index("run")) * ROWS
    for own, source in enumerate((theirs, mine)):
        g = half if own else 1 - half
        for which, plane in enumerate(plane_order()):
            cells = jnp.where(source[plane, cols, :] != 0, 0.0, 1.0)
            wide = jnp.concatenate([cells, cells], 1)
            wide = pltpu.roll(wide, LANES - first_row, 1)
            for y in range(ROWS):
                table[which, g, y] = jnp.broadcast_to(wide[:, y : y + 1], (COLS, LANES))


def both_planes(planes, beyond, faces, open_cells, put):
    column = lax.axis_index("column")
    core = lax.axis_index("core")
    sign = jnp.where(core == 0, 1.0, -1.0).astype(jnp.float32)
    wraps = ((column == 0) & (core == 0)) | ((column == 3) & (core == 1))
    for which in range(2):
        steps = [(1 - 2 * which) * HALF * math.sqrt(a) * sign for a in range(MA)]
        advance(
            wraps if which == 0 else None, steps, planes[which], planes[1 - which], beyond[which],
            *[face.at[which] for face in faces], open_cells.at[which], functools.partial(put, which),
        )


def first_kernel(
    outer_plane, inner_plane, outer_beyond, inner_beyond, y_back, y_next, z_back, z_next,
    mine, theirs, out_outer, out_inner, open_cells, *edges,
):
    open_table(mine, theirs, open_cells)

    def put(which, g, a, y, value):
        (out_outer, out_inner)[which][g, a, y] = value
        put_edges(g, a, y, value, *[edge.at[which] for edge in edges])

    both_planes(
        (outer_plane, inner_plane), (outer_beyond, inner_beyond), (y_back, y_next, z_back, z_next),
        open_cells, put,
    )


def tile_of(half, row):
    return half, slice(None), slice(None), pl.ds(row * COLS, COLS)


def plane_order():
    core = lax.axis_index("core")
    return core, 1 - core


def gather_blocks(field, blocks, arrived):
    copies = []
    for which, plane in enumerate(plane_order()):
        for half in range(2):
            for row in range(4):
                copies.append(
                    pltpu.make_async_copy(
                        field.at[plane].at[tile_of(half, row)],
                        blocks.at[half, row, :, which],
                        arrived.at[which, half, row],
                    )
                )
    for copy in copies:
        copy.start()
    for copy in copies:
        copy.wait()


def scatter_blocks(blocks, field, arrived):
    copies = []
    for which, plane in enumerate(plane_order()):
        for half in range(2):
            for row in range(4):
                copies.append(
                    pltpu.make_async_copy(
                        blocks.at[half, row, :, which],
                        field.at[plane].at[tile_of(half, row)],
                        arrived.at[which, half, row],
                    )
                )
    for copy in copies:
        copy.start()
    for copy in copies:
        copy.wait()


def three_parts(value):
    high = value.astype(jnp.bfloat16)
    rest = value - high.astype(jnp.float32)
    middle = rest.astype(jnp.bfloat16)
    low = (rest - middle.astype(jnp.float32)).astype(jnp.bfloat16)
    return high, middle, low


def second_kernel(
    outer_plane, inner_plane, outer_beyond, inner_beyond, y_back, y_next, z_back, z_next,
    open_cells, selector, weights, out, low, factors,
):
    def put(which, g, a, y, value):
        out[g, a, which, y] = value

    both_planes(
        (outer_plane, inner_plane), (outer_beyond, inner_beyond), (y_back, y_next, z_back, z_next),
        open_cells, put,
    )
    cells = 2 * 2 * ROWS * COLS
    lane = lax.broadcasted_iota(jnp.int32, (cells, LANES), 1)

    def plane(a):
        parts = [out[g, a, p].reshape(ROWS * COLS, LANES) for g in range(2) for p in range(2)]
        return jnp.concatenate(parts, 0)

    picked = jnp.zeros((PAD, cells), jnp.float32)
    for a in range(0, LOW_A, 2):
        paired = jnp.where(lane < LANES // 2, plane(a), pltpu.roll(plane(a + 1), LANES // 2, 1))
        for part in three_parts(paired):
            picked = picked + lax.dot_general(
                selector[a // 2], part, (((1,), (1,)), ((), ())), preferred_element_type=jnp.float32
            )
    low[...] = picked

    rate = jnp.zeros((BASIS_SIZE, cells), jnp.float32)
    values = low[0:BASIS_SIZE]
    for step in range(0, BASIS_SIZE, GROUP):
        count = min(GROUP, BASIS_SIZE - step)
        slot = factors.at[step // GROUP % 2]
        for i in range(0, count, 2):
            pair = [values * low[step + i + n : step + i + n + 1, :] for n in range(2)]
            slot[i * BASIS_SIZE : (i + 2) * BASIS_SIZE, :] = jnp.concatenate(pair, 0).astype(jnp.bfloat16)
        rate = rate + jnp.dot(
            weights[:, step * BASIS_SIZE : (step + count) * BASIS_SIZE],
            slot[0 : count * BASIS_SIZE, :],
            preferred_element_type=jnp.float32,
        )
    rate = jnp.concatenate([rate, jnp.zeros((PAD - BASIS_SIZE, cells), jnp.float32)], 0)
    rate_parts = three_parts(jnp.transpose(DTC * rate))
    for a in range(0, LOW_A, 2):
        lifted = jnp.zeros((cells, LANES), jnp.float32)
        for part in rate_parts:
            lifted = lifted + jnp.dot(part, selector[a // 2], preferred_element_type=jnp.float32)
        halves = (
            jnp.where(lane < LANES // 2, lifted, 0.0),
            jnp.where(lane < LANES // 2, pltpu.roll(lifted, LANES // 2, 1), 0.0),
        )
        for n, value in enumerate(halves):
            for g in range(2):
                for p in range(2):
                    at = (g * 2 + p) * ROWS * COLS
                    block = value[at : at + ROWS * COLS].reshape(ROWS, COLS, LANES)
                    out[g, a + n, p] = out[g, a + n, p] + block


def low_selector():
    rank = 0
    table = np.zeros((LOW_A // 2, PAD, LANES), np.float32)
    for a in range(MA):
        for b in range(MB):
            for c in range(MC):
                if a + b + c <= LDEG:
                    table[a // 2, rank, a % 2 * (LANES // 2) + b * MC + c] = 1.0
                    rank += 1
    return jnp.asarray(table, jnp.bfloat16)


VMEM = pl.BlockSpec(memory_space=pltpu.VMEM)
PARAMS = pltpu.CompilerParams(vmem_limit_bytes=16 << 20)
HBM = pl.BlockSpec(memory_space=pltpu.HBM)
COPY_SEMS = [pltpu.SemaphoreType.DMA((2, 2, 4))]


def f32(*shape):
    return jax.ShapeDtypeStruct(shape, jnp.float32)


PLANE = f32(2, MA, ROWS, COLS, LANES)
EDGES = f32(2, 2, MA, ROWS, LANES)


def surroundings(outer_plane, inner_plane, edges):
    y0, y7, z0, z7 = edges
    outer_beyond = send(outer_plane, outer())
    inner_beyond = send(inner_plane, inner())
    y_back = send(y7, along_y(1))
    y_next = send(y0, along_y(-1))
    z_back = send(z7, along_z(1))
    z0, inner_beyond = lax.optimization_barrier((z0, inner_beyond))
    z_next = send(z0, along_z(-1))
    return outer_beyond, inner_beyond, y_back, y_next, z_back, z_next


def call(kernel, out_shape, *operands, operand_space=VMEM, out_space=VMEM, scratch=()):
    single = not isinstance(out_shape, tuple)
    return pl.pallas_call(
        kernel,
        out_shape=out_shape,
        in_specs=[operand_space] * len(operands),
        out_specs=out_space if single else (out_space,) * len(out_shape),
        scratch_shapes=scratch,
        compiler_params=PARAMS,
    )(*operands)


def exchange(blocks):
    return lax.all_to_all(blocks, ("half", "row", "run"), 0, 0, tiled=True)


def body(field, kernel_table, obstacles):
    mine = obstacles.transpose(0, 2, 1)
    theirs = send(mine, other_half())
    tiles = f32(2, 4, 4, 2, ROWS, COLS, LANES)
    tiled = (2, 2, 4, ROWS, 4 * COLS, LANES)
    blocks = call(gather_blocks, tiles, field.reshape(tiled), operand_space=HBM, scratch=COPY_SEMS)
    state = exchange(blocks.reshape(BLOCKS, 2, ROWS, COLS, LANES))
    state, theirs = lax.optimization_barrier((state, theirs))

    outer_plane, inner_plane, *edges = call(
        split_kernel, (PLANE,) * 2 + (EDGES,) * 4, state.reshape(2, MA, 2, ROWS, COLS, LANES)
    )
    around = surroundings(outer_plane, inner_plane, edges)
    outer_plane, inner_plane, open_cells, *edges = call(
        first_kernel, (PLANE,) * 2 + (f32(2, 2, ROWS, COLS, LANES),) + (EDGES,) * 4,
        outer_plane, inner_plane, *around, mine, theirs,
    )
    around = surroundings(outer_plane, inner_plane, edges)
    cells = 2 * 2 * ROWS * COLS
    state = call(
        second_kernel, f32(2, MA, 2, ROWS, COLS, LANES),
        outer_plane, inner_plane, *around, open_cells, low_selector(), kernel_table.T,
        scratch=[
            pltpu.VMEM((PAD, cells), jnp.float32),
            pltpu.VMEM((2, GROUP * BASIS_SIZE, cells), jnp.bfloat16),
        ],
    )
    back = exchange(state.reshape(BLOCKS, 2, ROWS, COLS, LANES))
    result = call(
        scatter_blocks, f32(*tiled), back.reshape(tiles.shape), out_space=HBM, scratch=COPY_SEMS
    )
    return result.reshape(2, 8 * ROWS, 4 * COLS, LANES)


def solution(mesh):
    named = Mesh(mesh.devices.reshape(SIZES), AXES)
    cells = ("half", "column", "core")
    modes = ("row", "run")
    placed = (P(cells, None, None, modes), P(), P(cells, None, None))
    return jax.shard_map(
        body, mesh=named, in_specs=placed, out_specs=P(cells, None, None, modes), check_vma=False
    )
```

```python
import functools
import math

import jax
import jax.numpy as jnp
import numpy as np
from jax import lax
from jax.experimental import pallas as pl
from jax.experimental.pallas import tpu as pltpu
from jax.sharding import Mesh, PartitionSpec as P

MA = 16
MB = 16
MC = 8
LDEG = 7
BASIS_SIZE = 120
LANES = MB * MC
LOW_A = LDEG + 1
PAD = 128
CFL = 0.04
DTC = 0.2
HALF = 0.5 * CFL
CX = HALF * 2.0 * math.sqrt(MA)
CY = HALF * 2.0 * math.sqrt(MB)
CZ = HALF * 2.0 * math.sqrt(MC)
CENTER = 2.0 * (CX + CY + CZ)
ROWS = 8
COLS = 8
GROUP = 16
BLOCKS = 32

AXES = ("half", "column", "core", "row", "run")
SIZES = (2, 4, 2, 4, 4)


def pairs(move):
    out = []
    for source in np.ndindex(*SIZES):
        target = move(*source)
        out.append((int(np.ravel_multi_index(source, SIZES)), int(np.ravel_multi_index(target, SIZES))))
    return out


def outer():
    def move(half, column, core, row, run):
        place = (column * 2 + core + (1 if core else -1)) % 8
        return (half, place // 2, place % 2, row, run)

    return pairs(move)


def inner():
    return pairs(lambda half, column, core, row, run: (half, column, 1 - core, row, run))


def along_y(by):
    def move(half, column, core, row, run):
        place = (half * 4 + run + by) % 8
        return (place // 4, column, core, row, place % 4)

    return pairs(move)


def along_z(by):
    return pairs(lambda half, column, core, row, run: (half, column, core, (row + by) % 4, run))


def other_half():
    return pairs(lambda half, column, core, row, run: (1 - half, column, core, row, run))


def send(value, route):
    return lax.ppermute(value, AXES, route)


def ladder_rows():
    lane = lax.broadcasted_iota(jnp.int32, (COLS, LANES), 1)
    b = lane // MC
    c = lane % MC
    b_low = HALF * jnp.sqrt(b.astype(jnp.float32))
    b_high = jnp.where(b < MB - 1, HALF * jnp.sqrt((b + 1).astype(jnp.float32)), 0.0)
    c_low = HALF * jnp.sqrt(c.astype(jnp.float32))
    c_high = jnp.where(c < MC - 1, HALF * jnp.sqrt((c + 1).astype(jnp.float32)), 0.0)
    return b_low, b_high, c_low, c_high


def own_part(steps, here, beside, put):
    b_low, b_high, c_low, c_high = ladder_rows()
    depth = lax.broadcasted_iota(jnp.int32, (COLS, LANES), 0)
    at_start = depth == 0
    at_end = depth == COLS - 1

    def block(g, carry):
        for y in range(ROWS):
            for a in range(MA):
                f = here[g, a, y]
                zb = jnp.where(at_start, 0.0, pltpu.roll(f, 1, 0))
                zn = jnp.where(at_end, 0.0, pltpu.roll(f, COLS - 1, 0))
                if y == 0:
                    dy = across = here[g, a, y + 1]
                elif y == ROWS - 1:
                    across = here[g, a, y - 1]
                    dy = -across
                else:
                    dy = here[g, a, y + 1] - here[g, a, y - 1]
                    across = here[g, a, y + 1] + here[g, a, y - 1]
                dz = zn - zb
                change = CX * (beside[g, a, y] + across) + CZ * (zn + zb) - CENTER * f
                if a > 0:
                    change = change - steps[a] * beside[g, a - 1, y]
                if a + 1 < MA:
                    change = change - steps[a + 1] * beside[g, a + 1, y]
                change = change - b_low * pltpu.roll(dy, MC, 1)
                change = change - b_high * pltpu.roll(dy, LANES - MC, 1)
                change = change - c_low * pltpu.roll(dz, 1, 1)
                change = change - c_high * pltpu.roll(dz, LANES - 1, 1)
                put(g, a, y, change)
        return carry

    lax.fori_loop(0, 2, block, 0)


def advance(swap, steps, here, change, beyond, y_back, y_next, z_back, z_next, open_cells, ends, put):
    b_low, b_high, c_low, c_high = ladder_rows()
    depth = lax.broadcasted_iota(jnp.int32, (COLS, LANES), 0)
    at_start = depth == 0
    at_end = depth == COLS - 1

    def ladder(value, low, high, by):
        return low * pltpu.roll(value, by, 1) + high * pltpu.roll(value, LANES - by, 1)

    def block(g, carry):
        far = g if swap is None else jnp.where(swap, 1 - g, g)
        for a in range(MA):
            back, ahead = z_back[g, a], z_next[g, a]
            ends[0, a] = CZ * back + ladder(back, c_low, c_high, 1)
            ends[1, a] = CZ * ahead - ladder(ahead, c_low, c_high, 1)
        for y in range(ROWS):
            is_open = open_cells[g, y]
            for a in range(MA):
                total = change[g, a, y] + CX * beyond[far, a, y]
                if a > 0:
                    total = total + steps[a] * beyond[far, a - 1, y]
                if a + 1 < MA:
                    total = total + steps[a + 1] * beyond[far, a + 1, y]
                if y == 0:
                    back = y_back[g, a]
                    total = total + CY * back + ladder(back, b_low, b_high, MC)
                if y == ROWS - 1:
                    ahead = y_next[g, a]
                    total = total + CY * ahead - ladder(ahead, b_low, b_high, MC)
                last = jnp.where(at_end, ends[1, a, y : y + 1, :], 0.0)
                total = total + jnp.where(at_start, ends[0, a, y : y + 1, :], last)
                put(g, a, y, here[g, a, y] + is_open * total)
        return carry

    lax.fori_loop(0, 2, block, 0)


def put_edges(g, a, y, value, out_y0, out_y7, out_z0, out_z7):
    if y == 0:
        out_y0[g, a] = value
    if y == ROWS - 1:
        out_y7[g, a] = value
    out_z0[g, a, y : y + 1, :] = value[0:1]
    out_z7[g, a, y : y + 1, :] = value[COLS - 1 : COLS]


def split_kernel(state, out_outer, out_inner, *edges):
    def block(index, carry):
        g = index // MA
        a = index % MA
        for which, out in enumerate((out_outer, out_inner)):
            for y in range(ROWS):
                value = state[g, a, which, y]
                out[g, a, y] = value
                put_edges(g, a, y, value, *[edge.at[which] for edge in edges])
        return carry

    lax.fori_loop(0, 2 * MA, block, 0)


def open_table(mine, theirs, table):
    half = lax.axis_index("half")
    cols = pl.ds(pl.multiple_of(lax.axis_index("row") * COLS, COLS), COLS)
    first_row = (half * 4 + lax.axis_index("run")) * ROWS
    for own, source in enumerate((theirs, mine)):
        g = half if own else 1 - half
        for which, plane in enumerate(plane_order()):
            cells = jnp.where(source[plane, cols, :] != 0, 0.0, 1.0)
            wide = jnp.concatenate([cells, cells], 1)
            wide = pltpu.roll(wide, lax.rem(LANES - first_row, LANES), 1)
            for y in range(ROWS):
                table[which, g, y] = jnp.broadcast_to(wide[:, y : y + 1], (COLS, LANES))


def ladder_steps(which):
    sign = jnp.where(lax.axis_index("core") == 0, 1.0, -1.0).astype(jnp.float32)
    return [(1 - 2 * which) * HALF * math.sqrt(a) * sign for a in range(MA)]


def own_kernel(outer_plane, inner_plane, change):
    planes = (outer_plane, inner_plane)
    for which in range(2):

        def put(g, a, y, value):
            change[which, g, a, y] = value

        own_part(ladder_steps(which), planes[which], planes[1 - which], put)


def both_planes(planes, change, beyond, faces, open_cells, ends, put):
    column = lax.axis_index("column")
    core = lax.axis_index("core")
    wraps = ((column == 0) & (core == 0)) | ((column == 3) & (core == 1))
    for which in range(2):
        advance(
            wraps if which == 0 else None, ladder_steps(which), planes[which], change.at[which],
            beyond[which], *[face.at[which] for face in faces], open_cells.at[which], ends,
            functools.partial(put, which),
        )


def first_kernel(
    outer_plane, inner_plane, change, outer_beyond, inner_beyond, y_back, y_next, z_back, z_next,
    mine, theirs, out_outer, out_inner, open_cells, out_y0, out_y7, out_z0, out_z7, ends,
):
    edges = (out_y0, out_y7, out_z0, out_z7)
    open_table(mine, theirs, open_cells)

    def put(which, g, a, y, value):
        (out_outer, out_inner)[which][g, a, y] = value
        put_edges(g, a, y, value, *[edge.at[which] for edge in edges])

    both_planes(
        (outer_plane, inner_plane), change, (outer_beyond, inner_beyond),
        (y_back, y_next, z_back, z_next), open_cells, ends, put,
    )


def tile_of(half, row):
    return half, slice(None), slice(None), pl.ds(row * COLS, COLS)


def plane_order():
    core = lax.axis_index("core")
    return core, 1 - core


def gather_blocks(field, blocks, stage, arrived, stored):
    loads, stores = [], []
    for which, plane in enumerate(plane_order()):
        for half in range(2):
            for row in range(4):
                at = (which, half, row)
                loads.append(
                    pltpu.make_async_copy(
                        field.at[plane].at[tile_of(half, row)], stage.at[at], arrived.at[at]
                    )
                )
                stores.append(
                    pltpu.make_async_copy(stage.at[at], blocks.at[half, row, :, which], stored.at[at])
                )
    for load in loads:
        load.start()
    for load, store in zip(loads, stores):
        load.wait()
        store.start()
    for store in stores:
        store.wait()


def scatter_blocks(blocks, field, arrived):
    copies = []
    for which, plane in enumerate(plane_order()):
        for half in range(2):
            for row in range(4):
                copies.append(
                    pltpu.make_async_copy(
                        blocks.at[half, row, :, which],
                        field.at[plane].at[tile_of(half, row)],
                        arrived.at[which, half, row],
                    )
                )
    for copy in copies:
        copy.start()
    for copy in copies:
        copy.wait()


def three_parts(value):
    high = value.astype(jnp.bfloat16)
    rest = value - high.astype(jnp.float32)
    middle = rest.astype(jnp.bfloat16)
    low = (rest - middle.astype(jnp.float32)).astype(jnp.bfloat16)
    return high, middle, low


def second_kernel(
    outer_plane, inner_plane, change, outer_beyond, inner_beyond, y_back, y_next, z_back, z_next,
    open_cells, selector, weights, out, ends, low, factors,
):
    def put(which, g, a, y, value):
        out[g, a, which, y] = value

    both_planes(
        (outer_plane, inner_plane), change, (outer_beyond, inner_beyond),
        (y_back, y_next, z_back, z_next), open_cells, ends, put,
    )
    cells = 2 * 2 * ROWS * COLS
    lane = lax.broadcasted_iota(jnp.int32, (cells, LANES), 1)

    def plane(a):
        parts = [out[g, a, p].reshape(ROWS * COLS, LANES) for g in range(2) for p in range(2)]
        return jnp.concatenate(parts, 0)

    picked = jnp.zeros((PAD, cells), jnp.float32)
    for a in range(0, LOW_A, 2):
        paired = jnp.where(lane < LANES // 2, plane(a), pltpu.roll(plane(a + 1), LANES // 2, 1))
        for part in three_parts(paired):
            picked = picked + lax.dot_general(
                selector[a // 2], part, (((1,), (1,)), ((), ())), preferred_element_type=jnp.float32
            )
    low[...] = picked

    rate = jnp.zeros((BASIS_SIZE, cells), jnp.float32)
    values = low[0:BASIS_SIZE]
    for step in range(0, BASIS_SIZE, GROUP):
        count = min(GROUP, BASIS_SIZE - step)
        slot = factors.at[step // GROUP % 2]
        for i in range(0, count, 2):
            pair = [values * low[step + i + n : step + i + n + 1, :] for n in range(2)]
            slot[i * BASIS_SIZE : (i + 2) * BASIS_SIZE, :] = jnp.concatenate(pair, 0).astype(jnp.bfloat16)
        rate = rate + jnp.dot(
            weights[:, step * BASIS_SIZE : (step + count) * BASIS_SIZE],
            slot[0 : count * BASIS_SIZE, :],
            preferred_element_type=jnp.float32,
        )
    rate = jnp.concatenate([rate, jnp.zeros((PAD - BASIS_SIZE, cells), jnp.float32)], 0)
    rate_parts = three_parts(jnp.transpose(DTC * rate))
    for a in range(0, LOW_A, 2):
        lifted = jnp.zeros((cells, LANES), jnp.float32)
        for part in rate_parts:
            lifted = lifted + jnp.dot(part, selector[a // 2], preferred_element_type=jnp.float32)
        halves = (
            jnp.where(lane < LANES // 2, lifted, 0.0),
            jnp.where(lane < LANES // 2, pltpu.roll(lifted, LANES // 2, 1), 0.0),
        )
        for n, value in enumerate(halves):
            for g in range(2):
                for p in range(2):
                    at = (g * 2 + p) * ROWS * COLS
                    block = value[at : at + ROWS * COLS].reshape(ROWS, COLS, LANES)
                    out[g, a + n, p] = out[g, a + n, p] + block


def low_selector():
    rank = 0
    table = np.zeros((LOW_A // 2, PAD, LANES), np.float32)
    for a in range(MA):
        for b in range(MB):
            for c in range(MC):
                if a + b + c <= LDEG:
                    table[a // 2, rank, a % 2 * (LANES // 2) + b * MC + c] = 1.0
                    rank += 1
    return jnp.asarray(table, jnp.bfloat16)


VMEM = pl.BlockSpec(memory_space=pltpu.VMEM)
PARAMS = pltpu.CompilerParams(vmem_limit_bytes=16 << 20)
WHOLE = pltpu.CompilerParams(vmem_limit_bytes=61 << 20)
HBM = pl.BlockSpec(memory_space=pltpu.HBM)
COPY_SEMS = [pltpu.SemaphoreType.DMA((2, 2, 4))]


def f32(*shape):
    return jax.ShapeDtypeStruct(shape, jnp.float32)


PLANE = f32(2, MA, ROWS, COLS, LANES)
EDGES = f32(2, 2, MA, ROWS, LANES)
CHANGE = f32(2, 2, MA, ROWS, COLS, LANES)
ENDS = pltpu.VMEM((2, MA, ROWS, LANES), jnp.float32)


def surroundings(outer_plane, inner_plane, edges):
    y0, y7, z0, z7 = edges
    outer_beyond = send(outer_plane, outer())
    inner_beyond = send(inner_plane, inner())
    y_back = send(y7, along_y(1))
    y_next = send(y0, along_y(-1))
    z_back = send(z7, along_z(1))
    z0, inner_beyond = lax.optimization_barrier((z0, inner_beyond))
    z_next = send(z0, along_z(-1))
    return outer_beyond, inner_beyond, y_back, y_next, z_back, z_next


def call(kernel, out_shape, *operands, operand_space=VMEM, out_space=VMEM, scratch=(), params=PARAMS):
    single = not isinstance(out_shape, tuple)
    return pl.pallas_call(
        kernel,
        out_shape=out_shape,
        in_specs=[operand_space] * len(operands),
        out_specs=out_space if single else (out_space,) * len(out_shape),
        scratch_shapes=scratch,
        compiler_params=params,
    )(*operands)


def exchange(blocks):
    return lax.all_to_all(blocks, ("half", "row", "run"), 0, 0, tiled=True)


def body(field, kernel_table, obstacles):
    mine = obstacles.transpose(0, 2, 1)
    theirs = send(mine, other_half())
    tiles = f32(2, 4, 4, 2, ROWS, COLS, LANES)
    tiled = (2, 2, 4, ROWS, 4 * COLS, LANES)
    blocks = call(
        gather_blocks, tiles, field.reshape(tiled), operand_space=HBM, out_space=HBM, params=WHOLE,
        scratch=[pltpu.VMEM((2, 2, 4, 4, ROWS, COLS, LANES), jnp.float32)] + COPY_SEMS * 2,
    )
    state = exchange(blocks.reshape(BLOCKS, 2, ROWS, COLS, LANES))
    state, theirs = lax.optimization_barrier((state, theirs))

    outer_plane, inner_plane, *edges = call(
        split_kernel, (PLANE,) * 2 + (EDGES,) * 4, state.reshape(2, MA, 2, ROWS, COLS, LANES)
    )
    around = surroundings(outer_plane, inner_plane, edges)
    change = call(own_kernel, CHANGE, outer_plane, inner_plane)
    outer_plane, inner_plane, open_cells, *edges = call(
        first_kernel, (PLANE,) * 2 + (f32(2, 2, ROWS, COLS, LANES),) + (EDGES,) * 4,
        outer_plane, inner_plane, change, *around, mine, theirs, scratch=[ENDS],
    )
    around = surroundings(outer_plane, inner_plane, edges)
    change = call(own_kernel, CHANGE, outer_plane, inner_plane)
    cells = 2 * 2 * ROWS * COLS
    state = call(
        second_kernel, f32(2, MA, 2, ROWS, COLS, LANES),
        outer_plane, inner_plane, change, *around, open_cells, low_selector(), kernel_table.T,
        scratch=[
            ENDS,
            pltpu.VMEM((PAD, cells), jnp.float32),
            pltpu.VMEM((2, GROUP * BASIS_SIZE, cells), jnp.bfloat16),
        ],
    )
    back = exchange(state.reshape(BLOCKS, 2, ROWS, COLS, LANES))
    result = call(
        scatter_blocks, f32(*tiled), back.reshape(tiles.shape), out_space=HBM, scratch=COPY_SEMS
    )
    return result.reshape(2, 8 * ROWS, 4 * COLS, LANES)


def solution(mesh):
    named = Mesh(mesh.devices.reshape(SIZES), AXES)
    cells = ("half", "column", "core")
    modes = ("row", "run")
    placed = (P(cells, None, None, modes), P(), P(cells, None, None))
    return jax.shard_map(
        body, mesh=named, in_specs=placed, out_specs=P(cells, None, None, modes), check_vma=False
    )
```

```python
import functools
import math

import jax
import jax.numpy as jnp
import numpy as np
from jax import lax
from jax.experimental import pallas as pl
from jax.experimental.pallas import tpu as pltpu
from jax.sharding import Mesh, PartitionSpec as P

MA = 16
MB = 16
MC = 8
LDEG = 7
BASIS_SIZE = 120
LANES = MB * MC
LOW_A = LDEG + 1
PAD = 128
CFL = 0.04
DTC = 0.2
HALF = 0.5 * CFL
CX = HALF * 2.0 * math.sqrt(MA)
CY = HALF * 2.0 * math.sqrt(MB)
CZ = HALF * 2.0 * math.sqrt(MC)
CENTER = 2.0 * (CX + CY + CZ)
ROWS = 8
COLS = 8
GROUP = 16
BLOCKS = 32

AXES = ("half", "column", "core", "row", "run")
SIZES = (2, 4, 2, 4, 4)


def pairs(move):
    out = []
    for source in np.ndindex(*SIZES):
        target = move(*source)
        out.append((int(np.ravel_multi_index(source, SIZES)), int(np.ravel_multi_index(target, SIZES))))
    return out


def outer():
    def move(half, column, core, row, run):
        place = (column * 2 + core + (1 if core else -1)) % 8
        return (half, place // 2, place % 2, row, run)

    return pairs(move)


def inner():
    return pairs(lambda half, column, core, row, run: (half, column, 1 - core, row, run))


def along_y(by):
    def move(half, column, core, row, run):
        place = (half * 4 + run + by) % 8
        return (place // 4, column, core, row, place % 4)

    return pairs(move)


def along_z(by):
    return pairs(lambda half, column, core, row, run: (half, column, core, (row + by) % 4, run))


def other_half():
    return pairs(lambda half, column, core, row, run: (1 - half, column, core, row, run))


def send(value, route):
    return lax.ppermute(value, AXES, route)


def ladder_rows():
    lane = lax.broadcasted_iota(jnp.int32, (COLS, LANES), 1)
    b = lane // MC
    c = lane % MC
    b_low = HALF * jnp.sqrt(b.astype(jnp.float32))
    b_high = jnp.where(b < MB - 1, HALF * jnp.sqrt((b + 1).astype(jnp.float32)), 0.0)
    c_low = HALF * jnp.sqrt(c.astype(jnp.float32))
    c_high = jnp.where(c < MC - 1, HALF * jnp.sqrt((c + 1).astype(jnp.float32)), 0.0)
    return b_low, b_high, c_low, c_high


def own_part(steps, here, beside, put):
    b_low, b_high, c_low, c_high = ladder_rows()
    depth = lax.broadcasted_iota(jnp.int32, (COLS, LANES), 0)
    at_start = depth == 0
    at_end = depth == COLS - 1

    def block(g, carry):
        for y in range(ROWS):
            for a in range(MA):
                f = here[g, a, y]
                zb = jnp.where(at_start, 0.0, pltpu.roll(f, 1, 0))
                zn = jnp.where(at_end, 0.0, pltpu.roll(f, COLS - 1, 0))
                if y == 0:
                    dy = across = here[g, a, y + 1]
                elif y == ROWS - 1:
                    across = here[g, a, y - 1]
                    dy = -across
                else:
                    dy = here[g, a, y + 1] - here[g, a, y - 1]
                    across = here[g, a, y + 1] + here[g, a, y - 1]
                dz = zn - zb
                change = CX * (beside[g, a, y] + across) + CZ * (zn + zb) - CENTER * f
                if a > 0:
                    change = change - steps[a] * beside[g, a - 1, y]
                if a + 1 < MA:
                    change = change - steps[a + 1] * beside[g, a + 1, y]
                change = change - b_low * pltpu.roll(dy, MC, 1)
                change = change - b_high * pltpu.roll(dy, LANES - MC, 1)
                change = change - c_low * pltpu.roll(dz, 1, 1)
                change = change - c_high * pltpu.roll(dz, LANES - 1, 1)
                put(g, a, y, change)
        return carry

    lax.fori_loop(0, 2, block, 0)


def advance(swap, steps, here, change, beyond, y_back, y_next, z_back, z_next, open_cells, ends, put):
    b_low, b_high, c_low, c_high = ladder_rows()
    depth = lax.broadcasted_iota(jnp.int32, (COLS, LANES), 0)
    at_start = depth == 0
    at_end = depth == COLS - 1

    def ladder(value, low, high, by):
        return low * pltpu.roll(value, by, 1) + high * pltpu.roll(value, LANES - by, 1)

    def block(g, carry):
        far = g if swap is None else jnp.where(swap, 1 - g, g)
        for a in range(MA):
            back, ahead = z_back[g, a], z_next[g, a]
            ends[0, a] = CZ * back + ladder(back, c_low, c_high, 1)
            ends[1, a] = CZ * ahead - ladder(ahead, c_low, c_high, 1)
        for y in range(ROWS):
            is_open = open_cells[g, y]
            before, now = None, beyond[far, 0, y]
            for a in range(MA):
                after = beyond[far, a + 1, y] if a + 1 < MA else None
                total = change[g, a, y] + CX * now
                if before is not None:
                    total = total + steps[a] * before
                if after is not None:
                    total = total + steps[a + 1] * after
                before, now = now, after
                if y == 0:
                    back = y_back[g, a]
                    total = total + CY * back + ladder(back, b_low, b_high, MC)
                if y == ROWS - 1:
                    ahead = y_next[g, a]
                    total = total + CY * ahead - ladder(ahead, b_low, b_high, MC)
                last = jnp.where(at_end, ends[1, a, y : y + 1, :], 0.0)
                total = total + jnp.where(at_start, ends[0, a, y : y + 1, :], last)
                put(g, a, y, here[g, a, y] + is_open * total)
        return carry

    lax.fori_loop(0, 2, block, 0)


def put_edges(g, a, y, value, out_y0, out_y7, out_z0, out_z7):
    if y == 0:
        out_y0[g, a] = value
    if y == ROWS - 1:
        out_y7[g, a] = value
    out_z0[g, a, y : y + 1, :] = value[0:1]
    out_z7[g, a, y : y + 1, :] = value[COLS - 1 : COLS]


def split_kernel(state, out_outer, out_inner, out_y0, out_y7, out_z0, out_z7):
    def block(index, carry):
        g = index // MA
        a = index % MA
        for which, out in enumerate((out_outer, out_inner)):
            for y in range(ROWS):
                value = state[g, a, which, y]
                out[g, a, y] = value
                if y == 0:
                    out_y0[which, g, a] = value
                if y == ROWS - 1:
                    out_y7[which, g, a] = value
            out_z0[which, g, a] = state[g, a, which, :, 0, :]
            out_z7[which, g, a] = state[g, a, which, :, COLS - 1, :]
        return carry

    lax.fori_loop(0, 2 * MA, block, 0, unroll=4)


def open_table(mine, theirs, table):
    half = lax.axis_index("half")
    cols = pl.ds(pl.multiple_of(lax.axis_index("row") * COLS, COLS), COLS)
    first_row = (half * 4 + lax.axis_index("run")) * ROWS
    for own, source in enumerate((theirs, mine)):
        g = half if own else 1 - half
        for which, plane in enumerate(plane_order()):
            cells = jnp.where(source[plane, cols, :] != 0, 0.0, 1.0)
            wide = jnp.concatenate([cells, cells], 1)
            wide = pltpu.roll(wide, lax.rem(LANES - first_row, LANES), 1)
            for y in range(ROWS):
                table[which, g, y] = jnp.broadcast_to(wide[:, y : y + 1], (COLS, LANES))


def ladder_steps(which):
    sign = jnp.where(lax.axis_index("core") == 0, 1.0, -1.0).astype(jnp.float32)
    return [(1 - 2 * which) * HALF * math.sqrt(a) * sign for a in range(MA)]


def own_kernel(outer_plane, inner_plane, change):
    planes = (outer_plane, inner_plane)
    for which in range(2):

        def put(g, a, y, value):
            change[which, g, a, y] = value

        own_part(ladder_steps(which), planes[which], planes[1 - which], put)


def both_planes(planes, change, beyond, faces, open_cells, ends, put):
    column = lax.axis_index("column")
    core = lax.axis_index("core")
    wraps = ((column == 0) & (core == 0)) | ((column == 3) & (core == 1))
    for which in range(2):
        advance(
            wraps if which == 0 else None, ladder_steps(which), planes[which], change.at[which],
            beyond[which], *[face.at[which] for face in faces], open_cells.at[which], ends,
            functools.partial(put, which),
        )


def first_kernel(
    outer_plane, inner_plane, change, outer_beyond, inner_beyond, y_back, y_next, z_back, z_next,
    mine, theirs, out_outer, out_inner, open_cells, out_y0, out_y7, out_z0, out_z7, ends,
):
    edges = (out_y0, out_y7, out_z0, out_z7)
    open_table(mine, theirs, open_cells)

    def put(which, g, a, y, value):
        (out_outer, out_inner)[which][g, a, y] = value
        put_edges(g, a, y, value, *[edge.at[which] for edge in edges])

    both_planes(
        (outer_plane, inner_plane), change, (outer_beyond, inner_beyond),
        (y_back, y_next, z_back, z_next), open_cells, ends, put,
    )


def tile_of(half, row):
    return half, slice(None), slice(None), pl.ds(row * COLS, COLS)


def plane_order():
    core = lax.axis_index("core")
    return core, 1 - core


def gather_blocks(field, blocks, stage, arrived, stored):
    loads, stores = [], []
    for which, plane in enumerate(plane_order()):
        for half in range(2):
            for row in range(4):
                at = (which, half, row)
                loads.append(
                    pltpu.make_async_copy(
                        field.at[plane].at[tile_of(half, row)], stage.at[at], arrived.at[at]
                    )
                )
                stores.append(
                    pltpu.make_async_copy(stage.at[at], blocks.at[half, row, :, which], stored.at[at])
                )
    for load in loads:
        load.start()
    for load, store in zip(loads, stores):
        load.wait()
        store.start()
    for store in stores:
        store.wait()


def scatter_blocks(blocks, field, arrived):
    copies = []
    for which, plane in enumerate(plane_order()):
        for half in range(2):
            for row in range(4):
                copies.append(
                    pltpu.make_async_copy(
                        blocks.at[half, row, :, which],
                        field.at[plane].at[tile_of(half, row)],
                        arrived.at[which, half, row],
                    )
                )
    for copy in copies:
        copy.start()
    for copy in copies:
        copy.wait()


def three_parts(value):
    high = value.astype(jnp.bfloat16)
    rest = value - high.astype(jnp.float32)
    middle = rest.astype(jnp.bfloat16)
    low = (rest - middle.astype(jnp.float32)).astype(jnp.bfloat16)
    return high, middle, low


def second_kernel(
    outer_plane, inner_plane, change, outer_beyond, inner_beyond, y_back, y_next, z_back, z_next,
    open_cells, selector, weights, out, ends, low, factors,
):
    def put(which, g, a, y, value):
        out[g, a, which, y] = value

    both_planes(
        (outer_plane, inner_plane), change, (outer_beyond, inner_beyond),
        (y_back, y_next, z_back, z_next), open_cells, ends, put,
    )
    cells = 2 * 2 * ROWS * COLS
    lane = lax.broadcasted_iota(jnp.int32, (cells, LANES), 1)

    def plane(a):
        parts = [out[g, a, p].reshape(ROWS * COLS, LANES) for g in range(2) for p in range(2)]
        return jnp.concatenate(parts, 0)

    picked = jnp.zeros((PAD, cells), jnp.float32)
    for a in range(0, LOW_A, 2):
        paired = jnp.where(lane < LANES // 2, plane(a), pltpu.roll(plane(a + 1), LANES // 2, 1))
        for part in three_parts(paired):
            picked = picked + lax.dot_general(
                selector[a // 2], part, (((1,), (1,)), ((), ())), preferred_element_type=jnp.float32
            )
    low[...] = picked

    rate = jnp.zeros((BASIS_SIZE, cells), jnp.float32)
    values = low[0:BASIS_SIZE]
    for step in range(0, BASIS_SIZE, GROUP):
        count = min(GROUP, BASIS_SIZE - step)
        slot = factors.at[step // GROUP % 2]
        for i in range(0, count, 2):
            pair = [values * low[step + i + n : step + i + n + 1, :] for n in range(2)]
            slot[i * BASIS_SIZE : (i + 2) * BASIS_SIZE, :] = jnp.concatenate(pair, 0).astype(jnp.bfloat16)
        rate = rate + jnp.dot(
            weights[:, step * BASIS_SIZE : (step + count) * BASIS_SIZE],
            slot[0 : count * BASIS_SIZE, :],
            preferred_element_type=jnp.float32,
        )
    rate = jnp.concatenate([rate, jnp.zeros((PAD - BASIS_SIZE, cells), jnp.float32)], 0)
    rate_parts = three_parts(jnp.transpose(DTC * rate))[:2]
    for a in range(0, LOW_A, 2):
        lifted = jnp.zeros((cells, LANES), jnp.float32)
        for part in rate_parts:
            lifted = lifted + jnp.dot(part, selector[a // 2], preferred_element_type=jnp.float32)
        halves = (
            jnp.where(lane < LANES // 2, lifted, 0.0),
            jnp.where(lane < LANES // 2, pltpu.roll(lifted, LANES // 2, 1), 0.0),
        )
        for n, value in enumerate(halves):
            for g in range(2):
                for p in range(2):
                    at = (g * 2 + p) * ROWS * COLS
                    block = value[at : at + ROWS * COLS].reshape(ROWS, COLS, LANES)
                    out[g, a + n, p] = out[g, a + n, p] + block


def low_selector():
    rank = 0
    table = np.zeros((LOW_A // 2, PAD, LANES), np.float32)
    for a in range(MA):
        for b in range(MB):
            for c in range(MC):
                if a + b + c <= LDEG:
                    table[a // 2, rank, a % 2 * (LANES // 2) + b * MC + c] = 1.0
                    rank += 1
    return jnp.asarray(table, jnp.bfloat16)


VMEM = pl.BlockSpec(memory_space=pltpu.VMEM)
PARAMS = pltpu.CompilerParams(vmem_limit_bytes=16 << 20)
WHOLE = pltpu.CompilerParams(vmem_limit_bytes=61 << 20)
HBM = pl.BlockSpec(memory_space=pltpu.HBM)
COPY_SEMS = [pltpu.SemaphoreType.DMA((2, 2, 4))]


def f32(*shape):
    return jax.ShapeDtypeStruct(shape, jnp.float32)


PLANE = f32(2, MA, ROWS, COLS, LANES)
EDGES = f32(2, 2, MA, ROWS, LANES)
CHANGE = f32(2, 2, MA, ROWS, COLS, LANES)
ENDS = pltpu.VMEM((2, MA, ROWS, LANES), jnp.float32)


def surroundings(outer_plane, inner_plane, edges):
    y0, y7, z0, z7 = edges
    outer_beyond = send(outer_plane, outer())
    inner_beyond = send(inner_plane, inner())
    y_back = send(y7, along_y(1))
    y_next = send(y0, along_y(-1))
    z_back = send(z7, along_z(1))
    z0, inner_beyond = lax.optimization_barrier((z0, inner_beyond))
    z_next = send(z0, along_z(-1))
    return outer_beyond, inner_beyond, y_back, y_next, z_back, z_next


def call(kernel, out_shape, *operands, operand_space=VMEM, out_space=VMEM, scratch=(), params=PARAMS):
    single = not isinstance(out_shape, tuple)
    return pl.pallas_call(
        kernel,
        out_shape=out_shape,
        in_specs=[operand_space] * len(operands),
        out_specs=out_space if single else (out_space,) * len(out_shape),
        scratch_shapes=scratch,
        compiler_params=params,
    )(*operands)


def exchange(blocks):
    return lax.all_to_all(blocks, ("half", "row", "run"), 0, 0, tiled=True)


def body(field, kernel_table, obstacles):
    mine = obstacles.transpose(0, 2, 1)
    theirs = send(mine, other_half())
    tiles = f32(2, 4, 4, 2, ROWS, COLS, LANES)
    tiled = (2, 2, 4, ROWS, 4 * COLS, LANES)
    blocks = call(
        gather_blocks, tiles, field.reshape(tiled), operand_space=HBM, out_space=HBM, params=WHOLE,
        scratch=[pltpu.VMEM((2, 2, 4, 4, ROWS, COLS, LANES), jnp.float32)] + COPY_SEMS * 2,
    )
    state = exchange(blocks.reshape(BLOCKS, 2, ROWS, COLS, LANES))
    state, theirs = lax.optimization_barrier((state, theirs))

    outer_plane, inner_plane, *edges = call(
        split_kernel, (PLANE,) * 2 + (EDGES,) * 4, state.reshape(2, MA, 2, ROWS, COLS, LANES)
    )
    around = surroundings(outer_plane, inner_plane, edges)
    change = call(own_kernel, CHANGE, outer_plane, inner_plane)
    outer_plane, inner_plane, open_cells, *edges = call(
        first_kernel, (PLANE,) * 2 + (f32(2, 2, ROWS, COLS, LANES),) + (EDGES,) * 4,
        outer_plane, inner_plane, change, *around, mine, theirs, scratch=[ENDS],
    )
    around = surroundings(outer_plane, inner_plane, edges)
    change = call(own_kernel, CHANGE, outer_plane, inner_plane)
    cells = 2 * 2 * ROWS * COLS
    state = call(
        second_kernel, f32(2, MA, 2, ROWS, COLS, LANES),
        outer_plane, inner_plane, change, *around, open_cells, low_selector(), kernel_table.T,
        scratch=[
            ENDS,
            pltpu.VMEM((PAD, cells), jnp.float32),
            pltpu.VMEM((2, GROUP * BASIS_SIZE, cells), jnp.bfloat16),
        ],
    )
    back = exchange(state.reshape(BLOCKS, 2, ROWS, COLS, LANES))
    result = call(
        scatter_blocks, f32(*tiled), back.reshape(tiles.shape), out_space=HBM, scratch=COPY_SEMS
    )
    return result.reshape(2, 8 * ROWS, 4 * COLS, LANES)


def solution(mesh):
    named = Mesh(mesh.devices.reshape(SIZES), AXES)
    cells = ("half", "column", "core")
    modes = ("row", "run")
    placed = (P(cells, None, None, modes), P(), P(cells, None, None))
    return jax.shard_map(
        body, mesh=named, in_specs=placed, out_specs=P(cells, None, None, modes), check_vma=False
    )
```
